32 devices in a mesh: shard: 2 (over x), context: 8 (over z, y), tensor: 2 (over core).
Axes of the slice: x: 2, y: 2, z: 4, core: 2. Of those that a mesh axis runs over, the one named last changes fastest.
Arguments:
- tokens: bfloat16 [4096, 1024], P(('shard', 'context')), may hold values from -6 to 6
- positions: int32 [4096], P(('shard', 'context')), may hold values from 0 to 2047, as said below
- attention_gain: float32 [1024], replicated, may hold values from 0.25 to 1.75
- feedforward_gain: float32 [1024], replicated, may hold values from 0.25 to 1.75
- query_gain: float32 [64], replicated, may hold values from 0.5 to 2
- key_gain: float32 [64], replicated, may hold values from 0.5 to 2
- qkv_weight: bfloat16 [1024, 8, 256], P('shard', 'tensor'), may hold values from -0.1875 to 0.1875
- out_weight: bfloat16 [1024, 1024], P('tensor', 'shard'), may hold values from -1 to 1
- gate_up_weight: bfloat16 [1024, 2, 4608], P('shard', None, 'tensor'), may hold values from -0.1875 to 0.1875
- down_weight: bfloat16 [4608, 1024], P('tensor', 'shard'), may hold values from -0.09375 to 0.09375
- cotangent: bfloat16 [4096, 1024], P(('shard', 'context')), may hold values from -6 to 6
Outputs:
- output: bfloat16 [4096, 1024], P(('shard', 'context'))
- grad_tokens: float32 [4096, 1024], P(('shard', 'context'))
- grad_qkv_weight: float32 [1024, 8, 256], P(('shard', 'context'), 'tensor')
- grad_out_weight: float32 [1024, 1024], P('tensor', ('shard', 'context'))
- grad_gate_up_weight: float32 [1024, 2, 4608], P(('shard', 'context'), None, 'tensor')
- grad_down_weight: float32 [4608, 1024], P('tensor', ('shard', 'context'))
- grad_attention_gain: float32 [1024], replicated
- grad_feedforward_gain: float32 [1024], replicated
- grad_query_gain: float32 [64], replicated
- grad_key_gain: float32 [64], replicated
The draws below stay inside these ranges and needn't reach their ends.
Inputs may be any that keep to these rules, and one draw needn't show every extreme that they name: Rows s * 2048 to (s + 1) * 2048 - 1 hold each position of 0 to 2047 once; each aligned block of 256 rows holds 256 consecutive rising positions starting at a multiple of 256. Which block of a sequence holds which positions is drawn afresh for each sequence.
All inputs are finite; a program needn't handle non-finite values.
Results may differ from the reference program's by a relative error of at most 0.015.
Values may be sent and summed in bfloat16 or wider, within the bound.
No kernel may reach another device: no remote copies, remote signals or barrier semaphores. Data moves between devices by JAX's collectives and lax.ppermute only.
A program may use at most 128 MiB of HBM per device.

```python
import math
import jax
import jax.numpy as jnp
from jax import lax

D = 1024
H = 16
KV = 8
HD = 64
FF = 4608
TOK_DEV = 256
GROUP = 2
SEQ = 2048
TOKENS = 4096
N_SHARD = 2


def draw_positions(key, part):
    spans = SEQ // TOK_DEV
    sequences = TOKENS // SEQ

    def one_sequence(index):
        order = jax.random.permutation(jax.random.fold_in(key, index), spans).astype(jnp.int32)
        offsets = jnp.arange(TOK_DEV, dtype=jnp.int32)
        return (order[:, None] * TOK_DEV + offsets[None, :]).reshape(-1)
    return jax.vmap(one_sequence)(jnp.arange(sequences, dtype=jnp.int32)).reshape(-1).astype(jnp.int32)


def with_spikes(drawn, key, source, target, blocks, factor):
    owner, partner = [(jnp.arange(drawn.shape[position]) // (drawn.shape[position] // blocks)).reshape([-1 if axis == position else 1 for axis in range(drawn.ndim)]) for position in (source, target)]
    chosen = jax.random.permutation(key, blocks)[partner]
    strong = (owner == chosen) | (owner == (partner + blocks // 2) % blocks)
    return jnp.where(strong, factor * drawn, drawn)


def steps_of(key, dims, cuts, smallest, top_value):
    factor_of = 1.0
    for position, blocks in cuts:
        heights = jax.random.uniform(jax.random.fold_in(jax.random.fold_in(key, 6), position), (blocks,), jnp.float32, smallest / len(cuts), top_value / len(cuts))
        factor_of = factor_of * jnp.repeat(jnp.exp(heights), dims[position] // blocks).reshape((-1,) + (1,) * (len(dims) - 1 - position))
    return factor_of


def normal_values(stream_key, shape, spread, limit, cuts=(), kind=jnp.bfloat16):
    array = spread * jax.random.normal(stream_key, shape, jnp.float32)
    if cuts:
        array = array * steps_of(stream_key, shape, cuts, -0.22, 0.18)
    return jnp.clip(array, -limit, limit).astype(kind)


def heavy_noise(stream_key, shape, scale, bound, cuts, heavy, kind=jnp.bfloat16):
    entries = scale * jax.random.normal(stream_key, shape, jnp.float32)
    if cuts:
        entries = entries * steps_of(stream_key, shape, cuts, -0.22, 0.18)
    return jnp.clip(with_spikes(entries, jax.random.fold_in(stream_key, 3), *heavy), -bound, bound).astype(kind)


def setup_inputs(seed: int = 0) -> dict:
    keys = jax.random.split(jax.random.key(seed), 12)
    return {
        "tokens": normal_values(keys[0], (TOKENS, D), 1.0, 6.0, ((0, 16),)),
        "positions": draw_positions(jax.random.fold_in(keys[11], 71), 0),
        "attention_gain": jnp.clip(1.0 + 0.15 * jax.random.normal(keys[2], (D,), jnp.float32), 0.25, 1.75),
        "feedforward_gain": jnp.clip(1.0 + 0.15 * jax.random.normal(keys[3], (D,), jnp.float32), 0.25, 1.75),
        "query_gain": jnp.clip(jnp.exp(jax.random.uniform(keys[4], (HD,), jnp.float32, math.log(0.5), math.log(2.0))), 0.5, 2.0),
        "key_gain": jnp.clip(jnp.exp(jax.random.uniform(keys[5], (HD,), jnp.float32, math.log(0.5), math.log(2.0))), 0.5, 2.0),
        "qkv_weight": normal_values(keys[6], (D, KV, (GROUP + 2) * HD), D ** -0.5, 0.1875, ((0, 2), (1, 2))),
        "out_weight": normal_values(keys[7], (H * HD, D), (H * HD // 32) ** -0.5, 1.0, ((0, 2), (1, 2))),
        "gate_up_weight": normal_values(keys[8], (D, 2, FF), D ** -0.5, 0.1875, ((0, 2), (2, 2))),
        "down_weight": normal_values(keys[9], (FF, D), FF ** -0.5, 0.09375, ((0, 2), (1, 2))),
        "cotangent": heavy_noise(keys[10], (TOKENS, D), 1.0, 6.0, ((0, 16),), (0, 1, 16, 2.0)),
    }


EPSILON = 1e-05
THETA = 1000000.0

def rms_forward(values, gain):
    factor = lax.rsqrt(lax.optimization_barrier(jnp.mean(values * values, axis=-1, keepdims=True)) + EPSILON)
    return (values * factor * gain, factor)

def rms_backward(values, factor, gain, gradient):
    normal_unit = values * factor
    weighted = gradient * gain
    back = factor * (weighted - normal_unit * lax.optimization_barrier(jnp.mean(weighted * normal_unit, axis=-1, keepdims=True)))
    return (back, gradient * normal_unit)

def rope_tables(seq_positions, head_width):
    half_width = head_width // 2
    frequency = THETA ** (-2.0 * jnp.arange(half_width, dtype=jnp.float32) / head_width)
    angles = seq_positions.astype(jnp.float32)[:, None] * frequency[None, :]
    return (jnp.cos(angles), jnp.sin(angles))

def rotate(values, cos_table, sin_table):
    half_width = values.shape[-1] // 2
    leading = values[..., :half_width]
    trailing = values[..., half_width:]
    return jnp.concatenate([leading * cos_table - trailing * sin_table, trailing * cos_table + leading * sin_table], axis=-1)

def unrotate(gradient, cos_table, sin_table):
    half_width = gradient.shape[-1] // 2
    leading = gradient[..., :half_width]
    trailing = gradient[..., half_width:]
    return jnp.concatenate([leading * cos_table + trailing * sin_table, trailing * cos_table - leading * sin_table], axis=-1)

def attend_forward(query_rot, key_rot, value_rot, seq_positions, shift):
    length = key_rot.shape[0]
    block = min(length, 512)
    count = length // block
    query_blocks = query_rot.reshape(count, block * GROUP, HD)
    row_positions = jnp.repeat(seq_positions, GROUP).reshape(count, block * GROUP)
    inverse_root = HD ** (-0.5)

    def one_block(operands):
        query_rows, query_positions = operands
        scores = jnp.dot(query_rows, key_rot.T, preferred_element_type=jnp.float32) * inverse_root
        allowed = seq_positions[None, :] <= query_positions[:, None]
        weights = jnp.where(allowed, jnp.exp(scores - shift), 0.0)
        total = lax.optimization_barrier(jnp.sum(weights, axis=1))
        mixed = jnp.dot(weights.astype(jnp.bfloat16), value_rot, preferred_element_type=jnp.float32)
        return ((mixed / total[:, None]).astype(jnp.bfloat16), shift + jnp.log(total))
    attended, log_total = lax.map(one_block, (query_blocks, row_positions))
    return (attended.reshape(length, GROUP, HD), log_total.reshape(length, GROUP))

def attend_backward(query_rot, key_rot, value_rot, seq_positions, attended, grad_attended, log_total):
    length = key_rot.shape[0]
    block = min(length, 512)
    count = length // block
    inverse_root = HD ** (-0.5)
    delta = lax.optimization_barrier(jnp.sum(grad_attended.astype(jnp.float32) * attended.astype(jnp.float32), axis=-1))
    operands = (query_rot.reshape(count, block * GROUP, HD), jnp.repeat(seq_positions, GROUP).reshape(count, block * GROUP), grad_attended.reshape(count, block * GROUP, HD), log_total.reshape(count, block * GROUP), delta.reshape(count, block * GROUP))

    def one_block(carry, pieces):
        key_grad, value_grad = carry
        query_rows, query_positions, grad_rows, total_rows, delta_rows = pieces
        scores = jnp.dot(query_rows, key_rot.T, preferred_element_type=jnp.float32) * inverse_root
        allowed = seq_positions[None, :] <= query_positions[:, None]
        probs = jnp.where(allowed, jnp.exp(scores - total_rows[:, None]), 0.0)
        rounded = probs.astype(jnp.bfloat16)
        value_grad = value_grad + jnp.dot(rounded.T, grad_rows, preferred_element_type=jnp.float32)
        prob_grad = jnp.dot(grad_rows, value_rot.T, preferred_element_type=jnp.float32)
        score_grad = (probs * (prob_grad - delta_rows[:, None])).astype(jnp.bfloat16)
        query_grad = jnp.dot(score_grad, key_rot, preferred_element_type=jnp.float32) * inverse_root
        key_grad = key_grad + jnp.dot(score_grad.T, query_rows, preferred_element_type=jnp.float32) * inverse_root
        return ((key_grad, value_grad), query_grad)
    zeros = jnp.zeros((length, HD), jnp.float32)
    (key_grad, value_grad), query_grad = lax.scan(one_block, (zeros, zeros), operands)
    return (query_grad.reshape(length, GROUP, HD), key_grad, value_grad)

def reference(tokens, positions, attention_gain, feedforward_gain, query_gain, key_gain, qkv_weight, out_weight, gate_up_weight, down_weight, cotangent):
    flat_qkv = qkv_weight.reshape(D, KV * (GROUP + 2) * HD)
    flat_gate_up = gate_up_weight.reshape(D, 2 * FF)
    shift = math.sqrt(HD) * jnp.max(jnp.abs(query_gain)) * jnp.max(jnp.abs(key_gain))

    def one_sequence(carry, operands):
        seq_tokens, seq_positions, seq_cotangent = operands
        widened = seq_tokens.astype(jnp.float32)
        normed, scale_one = rms_forward(widened, attention_gain)
        first_input = normed.astype(jnp.bfloat16)
        projected = jnp.dot(first_input, flat_qkv, preferred_element_type=jnp.float32).reshape(SEQ, KV, GROUP + 2, HD)
        query_raw = projected[:, :, :GROUP]
        key_raw = projected[:, :, GROUP]
        value_raw = projected[:, :, GROUP + 1]
        query_normed, query_factor = rms_forward(query_raw, query_gain)
        key_normed, key_factor = rms_forward(key_raw, key_gain)
        cos_table, sin_table = rope_tables(seq_positions, HD)
        query_rot = rotate(query_normed, cos_table[:, None, None, :], sin_table[:, None, None, :]).astype(jnp.bfloat16)
        key_rot = rotate(key_normed, cos_table[:, None, :], sin_table[:, None, :]).astype(jnp.bfloat16)
        value_rot = value_raw.astype(jnp.bfloat16)
        query_heads = query_rot.transpose(1, 0, 2, 3)
        key_heads = key_rot.transpose(1, 0, 2)
        value_heads = value_rot.transpose(1, 0, 2)
        attended, log_total = lax.map(lambda pieces: attend_forward(pieces[0], pieces[1], pieces[2], seq_positions, shift), (query_heads, key_heads, value_heads))
        heads_out = attended.transpose(1, 0, 2, 3).reshape(SEQ, H * HD)
        hidden = widened + jnp.dot(heads_out, out_weight, preferred_element_type=jnp.float32)
        normed_two, scale_two = rms_forward(hidden, feedforward_gain)
        second_input = normed_two.astype(jnp.bfloat16)
        gate_up = jnp.dot(second_input, flat_gate_up, preferred_element_type=jnp.float32).reshape(SEQ, 2, FF)
        gating = gate_up[:, 0]
        upward = gate_up[:, 1]
        activated = (jax.nn.silu(gating) * upward).astype(jnp.bfloat16)
        output = (hidden + jnp.dot(activated, down_weight, preferred_element_type=jnp.float32)).astype(jnp.bfloat16)
        grad_down = jnp.dot(activated.T, seq_cotangent, preferred_element_type=jnp.float32)
        grad_activated = jnp.dot(seq_cotangent, down_weight.T, preferred_element_type=jnp.float32)
        sigmoid_gate = jax.nn.sigmoid(gating)
        grad_gating = grad_activated * upward * sigmoid_gate * (1.0 + gating * (1.0 - sigmoid_gate))
        grad_upward = grad_activated * gating * sigmoid_gate
        grad_gate_up = jnp.stack([grad_gating, grad_upward], axis=1).astype(jnp.bfloat16).reshape(SEQ, 2 * FF)
        grad_gate_weight = jnp.dot(second_input.T, grad_gate_up, preferred_element_type=jnp.float32)
        grad_second = jnp.dot(grad_gate_up, flat_gate_up.T, preferred_element_type=jnp.float32)
        back_two, gain_two_rows = rms_backward(hidden, scale_two, feedforward_gain, grad_second)
        grad_hidden = seq_cotangent.astype(jnp.float32) + back_two
        rounded_hidden_grad = grad_hidden.astype(jnp.bfloat16)
        grad_out = jnp.dot(heads_out.T, rounded_hidden_grad, preferred_element_type=jnp.float32)
        grad_attended = jnp.dot(rounded_hidden_grad, out_weight.T, preferred_element_type=jnp.float32).astype(jnp.bfloat16)
        grad_attended = grad_attended.reshape(SEQ, KV, GROUP, HD).transpose(1, 0, 2, 3)
        query_grad, key_grad, value_grad = lax.map(lambda pieces: attend_backward(pieces[0], pieces[1], pieces[2], seq_positions, pieces[3], pieces[4], pieces[5]), (query_heads, key_heads, value_heads, attended, grad_attended, log_total))
        query_grad = query_grad.transpose(1, 0, 2, 3)
        key_grad = key_grad.transpose(1, 0, 2)
        value_grad = value_grad.transpose(1, 0, 2)
        grad_query_norm = unrotate(query_grad, cos_table[:, None, None, :], sin_table[:, None, None, :])
        grad_key_norm = unrotate(key_grad, cos_table[:, None, :], sin_table[:, None, :])
        query_back, query_rows = rms_backward(query_raw, query_factor, query_gain, grad_query_norm)
        key_back, key_rows = rms_backward(key_raw, key_factor, key_gain, grad_key_norm)
        grad_projected = jnp.concatenate([query_back, key_back[:, :, None], value_grad[:, :, None]], axis=2)
        grad_projected = grad_projected.astype(jnp.bfloat16).reshape(SEQ, KV * (GROUP + 2) * HD)
        grad_qkv = jnp.dot(first_input.T, grad_projected, preferred_element_type=jnp.float32)
        grad_first = jnp.dot(grad_projected, flat_qkv.T, preferred_element_type=jnp.float32)
        back_one, gain_one_rows = rms_backward(widened, scale_one, attention_gain, grad_first)
        grad_tokens = grad_hidden + back_one
        updates = (grad_qkv, grad_out, grad_gate_weight, grad_down, lax.optimization_barrier(jnp.sum(gain_one_rows, axis=0)), lax.optimization_barrier(jnp.sum(gain_two_rows, axis=0)), lax.optimization_barrier(jnp.sum(query_rows, axis=(0, 1, 2))), lax.optimization_barrier(jnp.sum(key_rows, axis=(0, 1))))
        carry = tuple((previous + update for previous, update in zip(carry, updates)))
        return (carry, (output, grad_tokens))
    initial = (jnp.zeros((D, KV * (GROUP + 2) * HD), jnp.float32), jnp.zeros((H * HD, D), jnp.float32), jnp.zeros((D, 2 * FF), jnp.float32), jnp.zeros((FF, D), jnp.float32), jnp.zeros((D,), jnp.float32), jnp.zeros((D,), jnp.float32), jnp.zeros((HD,), jnp.float32), jnp.zeros((HD,), jnp.float32))
    sequences = (tokens.reshape(N_SHARD, SEQ, D), positions.reshape(N_SHARD, SEQ), cotangent.reshape(N_SHARD, SEQ, D))
    sums, results = lax.scan(one_sequence, initial, sequences)
    output = results[0].reshape(TOKENS, D)
    grad_tokens = results[1].reshape(TOKENS, D)
    return (output, grad_tokens, sums[0].reshape(D, KV, (GROUP + 2) * HD), sums[1], sums[2].reshape(D, 2, FF), sums[3], sums[4], sums[5], sums[6], sums[7])
```

```python
import math

import jax
import jax.numpy as jnp
from jax import lax
from jax.sharding import PartitionSpec as P

HD = 64
GROUP = 2


EPSILON = 1e-05
THETA = 1000000.0


BF = jnp.bfloat16
F32 = jnp.float32


def rms_forward(values, gain):
    factor = lax.rsqrt(jnp.mean(values * values, axis=-1, keepdims=True) + EPSILON)
    return (values * factor * gain, factor)


def rms_backward(values, factor, gain, gradient):
    normal_unit = values * factor
    weighted = gradient * gain
    back = factor * (
        weighted - normal_unit * jnp.mean(weighted * normal_unit, axis=-1, keepdims=True)
    )
    return (back, gradient * normal_unit)


def rope_tables(local_positions, head_width):
    half_width = head_width // 2
    frequency = THETA ** (-2.0 * jnp.arange(half_width, dtype=jnp.float32) / head_width)
    angles = local_positions.astype(jnp.float32)[:, None] * frequency[None, :]
    return (jnp.cos(angles), jnp.sin(angles))


def rotate(values, cos_table, sin_table):
    half_width = values.shape[-1] // 2
    leading = values[..., :half_width]
    trailing = values[..., half_width:]
    return jnp.concatenate(
        [leading * cos_table - trailing * sin_table, trailing * cos_table + leading * sin_table],
        axis=-1,
    )


def unrotate(gradient, cos_table, sin_table):
    half_width = gradient.shape[-1] // 2
    leading = gradient[..., :half_width]
    trailing = gradient[..., half_width:]
    return jnp.concatenate(
        [leading * cos_table + trailing * sin_table, trailing * cos_table - leading * sin_table],
        axis=-1,
    )


def swap(value, axis, step=1):
    count = lax.axis_size(axis)
    return lax.ppermute(value, axis, [(i, i ^ step) for i in range(count)])


def after(value, *earlier):
    return lax.optimization_barrier((value,) + earlier)[0]


def join(index, mine, other, axis):
    return jnp.where(
        index == 0,
        jnp.concatenate([mine, other], axis=axis),
        jnp.concatenate([other, mine], axis=axis),
    )


def half_of(value, index, axis):
    size = value.shape[axis] // 2
    return lax.dynamic_slice_in_dim(value, index * size, size, axis)


def sum_tensor(value):
    if lax.axis_size("tensor") == 2:
        return value + swap(value, "tensor")
    return lax.psum(value, "tensor")


def rows_of_pair(value, tensor):
    if lax.axis_size("tensor") == 2:
        got = swap(half_of(value, tensor, 0), "shard")
        return join(tensor, got, swap(got, "tensor"), 0)
    return swap(value, "shard")


def sum_of_pair(mine, other, tensor):
    if lax.axis_size("tensor") == 2:
        kept = half_of(other, tensor, 0) + swap(half_of(other, 1 - tensor, 0), "tensor")
        got = swap(kept.astype(BF), "shard")
        added = join(tensor, got, swap(got, "tensor"), 0)
        return (mine + swap(mine, "tensor")) + added.astype(F32)
    return lax.psum(mine + swap(other.astype(BF), "shard").astype(F32), "tensor")


def keep_half(value, bit, axis_name, step, axis):
    kept = lax.dynamic_index_in_dim(value, bit, axis, keepdims=False)
    sent = lax.dynamic_index_in_dim(value, 1 - bit, axis, keepdims=False)
    return kept + swap(sent.astype(BF), axis_name, step).astype(F32)


def scatter_context(value, context):
    count = value.shape[1]
    step = 1
    while count > 1:
        lead, _, rows, columns = value.shape
        value = value.reshape(lead, count // 2, 2, rows, columns)
        value = keep_half(value, (context // step) % 2, "context", step, 2)
        count //= 2
        step *= 2
    return value[:, 0]


def sum_all(value):
    value = value + swap(value, "shard")
    step = 1
    while step < lax.axis_size("context"):
        value = value + swap(value, "context", step)
        step *= 2
    return value


def per_device(
    tokens,
    positions,
    attention_gain,
    feedforward_gain,
    query_gain,
    key_gain,
    qkv_weight,
    out_weight,
    gate_up_weight,
    down_weight,
    cotangent,
):
    row_count, width = tokens.shape
    groups = qkv_weight.shape[1]
    spans = lax.axis_size("context")
    shard = lax.axis_index("shard")
    context = lax.axis_index("context")
    tensor = lax.axis_index("tensor")
    inverse_root = HD ** (-0.5)
    half_width = width // 2
    units = gate_up_weight.shape[2] // 2
    share = width // (2 * spans)
    zlow = (context // 2) % 2

    query_own = qkv_weight[:, :, : GROUP * HD].reshape(half_width, groups * GROUP * HD)
    pair_own = qkv_weight[:, :, GROUP * HD :].reshape(half_width, groups * 2 * HD)
    pair_other = swap(pair_own, "shard")
    query_other = swap(after(query_own, pair_other), "shard")
    out_other = swap(after(out_weight, query_other), "shard")
    units_own = half_of(gate_up_weight, shard, 2).transpose(1, 0, 2)
    units_sent = half_of(gate_up_weight, 1 - shard, 2).transpose(1, 0, 2)
    units_part = lax.dynamic_index_in_dim(units_sent, zlow, 0, keepdims=False)
    units_got = swap(after(units_part, out_other), "shard")
    units_rest = swap(units_got, "context", 2)
    down_own = half_of(down_weight, shard, 0)
    down_part = half_of(half_of(down_weight, 1 - shard, 0), zlow, 0)
    down_got = swap(after(down_part, units_got), "shard")
    down_rest = swap(down_got, "context", 2)
    cotangent_other = rows_of_pair(after(cotangent, down_got), tensor)

    gate_other = jnp.where(zlow == 0, units_got, units_rest)
    up_other = jnp.where(zlow == 0, units_rest, units_got)
    gate_full = join(shard, units_own[0], gate_other, 0)
    up_full = join(shard, units_own[1], up_other, 0)
    down_full = join(shard, down_own, join(zlow, down_got, down_rest, 0), 1)
    out_full = join(shard, out_weight, out_other, 1)

    widened = tokens.astype(F32)
    normed, scale_one = rms_forward(widened, attention_gain)
    first_input = normed.astype(BF)
    first_own = half_of(first_input, shard, 1)
    first_other = half_of(first_input, 1 - shard, 1)

    def project(own, other):
        return jnp.dot(first_own, own, preferred_element_type=F32) + jnp.dot(
            first_other, other, preferred_element_type=F32
        )

    cos_table, sin_table = rope_tables(positions, HD)
    pair_raw = project(pair_own, pair_other).reshape(row_count, groups, 2 * HD)
    key_raw = pair_raw[:, :, :HD]
    value_raw = pair_raw[:, :, HD:]
    key_normed, key_factor = rms_forward(key_raw, key_gain)
    key_rot = rotate(key_normed, cos_table[:, None, :], sin_table[:, None, :]).astype(BF)
    key_value = jnp.concatenate([key_rot, value_raw.astype(BF)], axis=-1)
    key_value = key_value.reshape(row_count, groups * 2 * HD)
    query_raw = project(query_own, query_other).reshape(row_count, groups, GROUP, HD)
    query_normed, query_factor = rms_forward(query_raw, query_gain)
    query_rot = rotate(
        query_normed, cos_table[:, None, None, :], sin_table[:, None, None, :]
    ).astype(BF)
    query_rows = [
        jnp.concatenate([query_rot[:, member, g] for g in range(GROUP)], axis=0)
        for member in range(groups)
    ]
    shift = math.sqrt(HD) * jnp.max(jnp.abs(query_gain)) * jnp.max(jnp.abs(key_gain))

    lanes = key_value.shape[1]
    high = (positions // 256).astype(BF)
    low = (positions % 256).astype(BF)
    place = jnp.zeros((16, max(lanes, row_count)), BF)
    place = place.at[0, :row_count].set(high).at[1, :row_count].set(low)
    if lanes < row_count:
        place = place.reshape(-1, lanes)
    payload = jnp.concatenate([key_value, place], axis=0)
    near = [payload] + [swap(payload, "context", k) for k in range(2, spans, 2)]
    far = [swap(piece, "context", 1) for piece in near]

    def opened(pieces):
        spots = []
        for piece in pieces:
            place = piece[row_count:].reshape(16, -1)[:2, :row_count].astype(jnp.int32)
            spots.append(place[0] * 256 + place[1])
        rows = jnp.concatenate([piece[:row_count] for piece in pieces], axis=0)
        return (rows, jnp.concatenate(spots))

    sets = [opened(near), opened(far)]
    row_positions = jnp.concatenate([positions] * GROUP)

    totals = [0.0] * groups
    sums = [0.0] * groups
    for rows, spots in sets:
        allowed = spots[None, :] <= row_positions[:, None]
        for member in range(groups):
            key_rows = rows[:, member * 2 * HD : member * 2 * HD + HD]
            value_rows = rows[:, member * 2 * HD + HD : (member + 1) * 2 * HD]
            scores = (
                jnp.dot(query_rows[member], key_rows.T, preferred_element_type=F32) * inverse_root
            )
            weights = jnp.where(allowed, jnp.exp(scores - shift), 0.0)
            totals[member] = totals[member] + jnp.sum(weights, axis=1)
            sums[member] = sums[member] + jnp.dot(
                weights.astype(BF), value_rows, preferred_element_type=F32
            )
    attended = [(sums[m] / totals[m][:, None]).astype(BF) for m in range(groups)]
    log_total = [shift + jnp.log(totals[m]) for m in range(groups)]
    heads_out = jnp.concatenate(
        [
            attended[m][g * row_count : (g + 1) * row_count]
            for m in range(groups)
            for g in range(GROUP)
        ],
        axis=1,
    )
    attn_part = jnp.dot(heads_out, out_full, preferred_element_type=F32)
    hidden = widened + sum_tensor(attn_part)

    normed_two, scale_two = rms_forward(hidden, feedforward_gain)
    second_input = normed_two.astype(BF)
    second_other = rows_of_pair(second_input, tensor)

    def feed_forward(rows, cotangent_rows):
        gating = jnp.dot(rows, gate_full, preferred_element_type=F32)
        upward = jnp.dot(rows, up_full, preferred_element_type=F32)
        activated = (jax.nn.silu(gating) * upward).astype(BF)
        out_rows = jnp.dot(activated, down_full, preferred_element_type=F32)
        grad_activated = jnp.dot(cotangent_rows, down_full.T, preferred_element_type=F32)
        sigmoid_gate = jax.nn.sigmoid(gating)
        grad_gating = (
            grad_activated * upward * sigmoid_gate * (1.0 + gating * (1.0 - sigmoid_gate))
        ).astype(BF)
        grad_upward = (grad_activated * gating * sigmoid_gate).astype(BF)
        grad_rows = jnp.dot(grad_gating, gate_full.T, preferred_element_type=F32) + jnp.dot(
            grad_upward, up_full.T, preferred_element_type=F32
        )
        return (activated, grad_gating, grad_upward, out_rows, grad_rows)

    mine = feed_forward(second_input, cotangent)
    theirs = feed_forward(second_other, cotangent_other)
    grad_second = sum_of_pair(mine[4], theirs[4], tensor)
    output = (hidden + sum_of_pair(mine[3], theirs[3], tensor)).astype(BF)
    activated, grad_gating, grad_upward = (
        jnp.concatenate([mine[i], theirs[i]], axis=0) for i in range(3)
    )
    second_rows = jnp.concatenate([second_input, second_other], axis=0)
    cotangent_rows = jnp.concatenate([cotangent, cotangent_other], axis=0)

    def scatter_units(rows, unit_rows):
        whole = jnp.dot(rows.T, unit_rows, preferred_element_type=F32)
        part = scatter_context(whole.reshape(2, spans, share, units), context)
        kept = lax.dynamic_index_in_dim(part, shard, 0, keepdims=False)
        sent = lax.dynamic_index_in_dim(part, 1 - shard, 0, keepdims=False)
        return join(shard, kept, swap(sent.astype(BF), "shard").astype(F32), 1)

    grad_down_weight = scatter_units(cotangent_rows, activated).T
    grad_gate_up_weight = jnp.stack(
        [scatter_units(second_rows, grad_gating), scatter_units(second_rows, grad_upward)], axis=1
    )

    back_two, gain_two_rows = rms_backward(hidden, scale_two, feedforward_gain, grad_second)
    grad_hidden = cotangent.astype(F32) + back_two
    gain_two_part = jnp.sum(gain_two_rows, axis=0)
    rounded_hidden_grad = grad_hidden.astype(BF)
    grad_heads = jnp.dot(rounded_hidden_grad, out_full.T, preferred_element_type=F32).astype(BF)

    def scatter_both(whole, columns):
        part = keep_half(whole.reshape(2, spans, share, columns), shard, "shard", 1, 0)
        return scatter_context(part[None], context)[0]

    grad_out_whole = jnp.dot(rounded_hidden_grad.T, heads_out, preferred_element_type=F32)
    grad_out_weight = scatter_both(grad_out_whole, heads_out.shape[1]).T

    grad_rows = [
        jnp.concatenate(
            [
                grad_heads[:, (m * GROUP + g) * HD : (m * GROUP + g + 1) * HD]
                for g in range(GROUP)
            ],
            axis=0,
        )
        for m in range(groups)
    ]
    delta = [
        jnp.sum(grad_rows[m].astype(F32) * attended[m].astype(F32), axis=-1) for m in range(groups)
    ]
    query_grad = [0.0] * groups

    def sweep(rows, spots):
        allowed = spots[None, :] <= row_positions[:, None]
        pieces = []
        for member in range(groups):
            key_rows = rows[:, member * 2 * HD : member * 2 * HD + HD]
            value_rows = rows[:, member * 2 * HD + HD : (member + 1) * 2 * HD]
            scores = (
                jnp.dot(query_rows[member], key_rows.T, preferred_element_type=F32) * inverse_root
            )
            probs = jnp.where(allowed, jnp.exp(scores - log_total[member][:, None]), 0.0)
            value_grad = jnp.dot(
                probs.astype(BF).T, grad_rows[member], preferred_element_type=F32
            )
            prob_grad = jnp.dot(grad_rows[member], value_rows.T, preferred_element_type=F32)
            score_grad = (probs * (prob_grad - delta[member][:, None])).astype(BF)
            query_grad[member] = query_grad[member] + (
                jnp.dot(score_grad, key_rows, preferred_element_type=F32) * inverse_root
            )
            key_grad = (
                jnp.dot(score_grad.T, query_rows[member], preferred_element_type=F32)
                * inverse_root
            )
            pieces += [key_grad, value_grad]
        return jnp.concatenate(pieces, axis=1)

    far_grad = swap(sweep(*sets[1]).astype(BF), "context", 1)
    near_grad = sweep(*sets[0])
    near_grad = near_grad + far_grad.astype(F32)
    near_grad = near_grad.reshape(spans // 2, row_count, groups * 2 * HD)
    kv_grad = near_grad[0]
    for k in range(1, spans // 2):
        kv_grad = kv_grad + swap(near_grad[k].astype(BF), "context", 2 * k).astype(F32)
    kv_grad = kv_grad.reshape(row_count, groups, 2 * HD)

    query_grad = jnp.stack(query_grad).reshape(groups, GROUP, row_count, HD).transpose(2, 0, 1, 3)
    key_grad = kv_grad[:, :, :HD]
    value_grad = kv_grad[:, :, HD:]
    grad_query_norm = unrotate(query_grad, cos_table[:, None, None, :], sin_table[:, None, None, :])
    grad_key_norm = unrotate(key_grad, cos_table[:, None, :], sin_table[:, None, :])
    query_back, query_gain_rows = rms_backward(query_raw, query_factor, query_gain, grad_query_norm)
    key_back, key_gain_rows = rms_backward(key_raw, key_factor, key_gain, grad_key_norm)
    grad_query = query_back.astype(BF).reshape(row_count, -1)
    grad_pair = jnp.concatenate([key_back, value_grad], axis=-1).astype(BF).reshape(row_count, -1)

    def back(query_part, pair_part):
        return jnp.dot(grad_query, query_part.T, preferred_element_type=F32) + jnp.dot(
            grad_pair, pair_part.T, preferred_element_type=F32
        )

    first_part = join(shard, back(query_own, pair_own), back(query_other, pair_other), 1)
    grad_first = sum_tensor(first_part)
    back_one, gain_one_rows = rms_backward(widened, scale_one, attention_gain, grad_first)
    grad_tokens = grad_hidden + back_one
    gain_one_part = jnp.sum(gain_one_rows, axis=0)

    query_columns = grad_query.shape[1]
    pair_columns = grad_pair.shape[1]
    query_whole = jnp.dot(first_input.T, grad_query, preferred_element_type=F32)
    pair_whole = jnp.dot(first_input.T, grad_pair, preferred_element_type=F32)
    query_scattered = scatter_both(query_whole, query_columns)
    pair_part = scatter_context(pair_whole.reshape(2, spans, share, pair_columns), context)
    pair_scattered = keep_half(pair_part, shard, "shard", 1, 0)
    grad_qkv_weight = jnp.concatenate(
        [
            query_scattered.reshape(share, groups, GROUP * HD),
            pair_scattered.reshape(share, groups, 2 * HD),
        ],
        axis=-1,
    )

    head_gains = sum_tensor(
        jnp.concatenate(
            [jnp.sum(query_gain_rows, axis=(0, 1, 2)), jnp.sum(key_gain_rows, axis=(0, 1))]
        )
    )
    gains = sum_all(jnp.concatenate([gain_one_part, gain_two_part, head_gains]))
    return (
        output,
        grad_tokens,
        grad_qkv_weight,
        grad_out_weight,
        grad_gate_up_weight,
        grad_down_weight,
        gains[:width],
        gains[width : 2 * width],
        gains[2 * width : 2 * width + HD],
        gains[2 * width + HD :],
    )


def solution(mesh):
    placed = (
        P(("shard", "context"), None),
        P(("shard", "context")),
        P(),
        P(),
        P(),
        P(),
        P("shard", "tensor", None),
        P("tensor", "shard"),
        P("shard", None, "tensor"),
        P("tensor", "shard"),
        P(("shard", "context"), None),
    )
    return jax.shard_map(
        per_device,
        mesh=mesh,
        in_specs=placed,
        out_specs=(
            P(("shard", "context"), None),
            P(("shard", "context"), None),
            P(("shard", "context"), "tensor", None),
            P("tensor", ("shard", "context")),
            P(("shard", "context"), None, "tensor"),
            P("tensor", ("shard", "context")),
            P(),
            P(),
            P(),
            P(),
        ),
        check_vma=False,
    )
```
